32 devices in a mesh: groups: 2 (over y), tensor: 4 (over z), query: 2 (over x), dp: 2 (over core).
Axes of the slice: x: 2, y: 2, z: 4, core: 2. Of those that a mesh axis runs over, the one named last changes fastest.
Arguments:
- features: bfloat16 [2048, 8192], P(('groups', 'dp'), 'query'), parts along dimension 0, may hold values from -6 to 6
- up_weight: bfloat16 [8192, 28672], P(('query', 'dp'), 'tensor'), may hold values from -0.09375 to 0.09375
- out_grad: bfloat16 [2048, 28672], P(('groups', 'dp'), 'tensor'), parts along dimension 0, may hold values from -6 to 6
- left_factors: bfloat16 [16, 32, 28672], P('query', None, 'tensor'), may hold values from -0.03125 to 0.03125
- right_factors: bfloat16 [16, 32, 8192], P('query', None, 'tensor'), may hold values from -0.0625 to 0.0625
- token_ids: int32 [2048], P(('groups', 'dp')), parts along dimension 0, may hold values from 0 to 15, never falling along the last dimension, each value on 1 to 128 neighbouring positions
- query_ids: int32 [2, 8], P('query'), may hold values from 0 to 7, each once within a row
Outputs:
- input_grad: bfloat16 [2048, 8192], P(('groups', 'dp'), ('query', 'tensor')), parts along dimension 0
- scores: float32 [32, 16], P('groups', 'query'), parts along dimension 0
The draws below stay inside these ranges and needn't reach their ends.
There are 2 independent parts, one for each index of `groups`. The reference program is written for one: setup_inputs(seed, part) draws one part's arguments, and reference() takes and returns one part's arrays. A program takes and returns all parts, laid end to end along the dimension named above; an argument that names none is the same for every part. Nothing has to cross between parts.
Inputs may be any that keep to these rules, and one draw needn't show every extreme that they name: token_ids never fall along the tokens; every example has at least one token. `query_ids`: each row is a permutation of the numbers below 8.
All inputs are finite; a program needn't handle non-finite values.
Results may differ from the reference program's by a relative error of at most 0.0049.
Values may be sent and summed in bfloat16 or wider, within the bound.
A program may use at most 192 MiB of HBM per device.

```python
import math
import jax
import jax.numpy as jnp
import numpy as np
from jax import lax

D = 8192
FF = 28672
R = 32
QPD = 8
EXAMPLES = 16
QSHARDS = 2
QUERIES = 16
TOKENS = 1024


def with_spikes(array, stream_key, source, target, parts, factor):
    owner, partner = [(jnp.arange(array.shape[position]) // (array.shape[position] // parts)).reshape([-1 if axis == position else 1 for axis in range(array.ndim)]) for position in (source, target)]
    chosen = jax.random.permutation(stream_key, parts)[partner]
    strong = (owner == chosen) | (owner == (partner + parts // 2) % parts)
    return jnp.where(strong, factor * array, array)


def levels(own_key, dims, cuts, least, top_value):
    def one(position, blocks):
        heights = jax.random.uniform(jax.random.fold_in(jax.random.fold_in(own_key, 6), position), (blocks,), jnp.float32, least / len(cuts), top_value / len(cuts))
        return jnp.repeat(jnp.exp(heights), dims[position] // blocks).reshape((-1,) + (1,) * (len(dims) - position - 1))

    factor_of = one(*cuts[0])
    for cut in cuts[1:]:
        factor_of = factor_of * one(*cut)
    return factor_of


def split_up(number_of, total, limit, skew):
    loads = [(1 << 20) // math.isqrt(standing ** skew) + 1 for standing in range(2, number_of + 1)]
    surplus, given = total - limit - (number_of - 1), [1] * (number_of - 1)
    while surplus > 0:
        movable = [i for i in range(number_of - 1) if given[i] < limit]
        whole, budget = sum([loads[i] for i in movable]), surplus
        for i in movable:
            addition = min(limit - given[i], max(1, budget * loads[i] // whole), surplus)
            given[i] = given[i] + addition
            surplus = surplus - addition
    return np.array([limit] + given)


def uneven(stream_key, amount, total, reach, lean):
    if amount == 2:
        one = jax.random.randint(stream_key, (), max(1, total - reach), min(reach, total - 1) + 1)
        return jnp.stack([one, total - one])
    sizes = jnp.asarray(split_up(amount, total, reach, lean), jnp.int32)
    pairs = (amount - 1) // 2
    giver, receiver = sizes[1:1 + 2 * pairs:2], sizes[2:2 + 2 * pairs:2]
    room = jnp.minimum(giver - 1, reach - receiver)
    moved = jax.random.randint(jax.random.fold_in(stream_key, 1), (pairs,), 0, 1 << 20) % (room + 1)
    sizes = sizes.at[1:1 + 2 * pairs:2].set(giver - moved).at[2:2 + 2 * pairs:2].set(receiver + moved)
    return sizes[jax.random.permutation(jax.random.fold_in(stream_key, 2), amount)]


def normal_values(own_key, shape, spread, reach, cuts=(), held_as=jnp.bfloat16):
    values = jax.random.normal(own_key, shape, jnp.float32) * spread
    if len(cuts) > 0:
        values = levels(own_key, shape, cuts, -0.22, 0.18) * values
    return jnp.clip(values, min=-reach, max=reach).astype(held_as)


def noise_with(own_key, dims, deviation, most, shards, heavy, kind=jnp.bfloat16):
    result = deviation * jax.random.normal(own_key, dims, jnp.float32)
    if shards:
        result = result * levels(own_key, dims, shards, -0.22, 0.18)
    return jnp.clip(with_spikes(result, jax.random.fold_in(own_key, 3), *heavy), -most, most).astype(kind)


def setup_inputs(seed: int = 0, part: int = 0) -> dict:
    arg_keys = jax.random.split(jax.random.key(seed), 8)
    part_keys = jax.random.split(jax.random.fold_in(arg_keys[7], part), 8)
    features = normal_values(part_keys[0], (TOKENS, D), 1.0, 6.0, ((0, 2), (1, 2)))
    up_weight = noise_with(arg_keys[1], (D, FF), D ** -0.5, 0.09375, ((0, 4), (1, 4)), (1, 0, 4, 2.0))
    out_grad = normal_values(part_keys[2], (TOKENS, FF), 1.0, 6.0, ((0, 2), (1, 4)))
    left_factors = normal_values(arg_keys[3], (QUERIES, R, FF), FF ** -0.5, 0.03125, ((0, 2), (2, 4)))
    right_factors = normal_values(arg_keys[4], (QUERIES, R, D), D ** -0.5, 0.0625, ((0, 2), (2, 4)))
    token_ids = jnp.searchsorted(jnp.cumsum(uneven(part_keys[5], EXAMPLES, TOKENS, 2 * TOKENS // EXAMPLES, 1)), jnp.arange(TOKENS), side="right").astype(jnp.int32)
    query_ids = jax.vmap(lambda own: jax.random.permutation(own, QPD))(jax.random.split(arg_keys[6], QSHARDS)).reshape((QSHARDS, QPD)).astype(jnp.int32)
    return {"features": features, "up_weight": up_weight, "out_grad": out_grad, "left_factors": left_factors, "right_factors": right_factors, "token_ids": token_ids, "query_ids": query_ids}


def reference(features, up_weight, out_grad, left_factors, right_factors, token_ids, query_ids):
    preact = jnp.dot(features, up_weight, preferred_element_type=jnp.float32)
    sigmoid_value = jax.nn.sigmoid(preact)
    grad_rows = (out_grad.astype(jnp.float32) * sigmoid_value * (1.0 + preact * (1.0 - sigmoid_value))).astype(jnp.bfloat16)
    input_grad = lax.dot_general(grad_rows, up_weight, (((1,), (1,)), ((), ())), preferred_element_type=jnp.float32).astype(jnp.bfloat16)
    left_proj = lax.dot_general(grad_rows, left_factors.reshape(QUERIES * R, FF), (((1,), (1,)), ((), ())), preferred_element_type=jnp.float32)
    right_proj = lax.dot_general(features, right_factors.reshape(QUERIES * R, D), (((1,), (1,)), ((), ())), preferred_element_type=jnp.float32)
    per_token = (left_proj * right_proj).reshape(TOKENS, QUERIES, R).sum(axis=-1)
    membership = (token_ids[None, :] == jnp.arange(EXAMPLES, dtype=jnp.int32)[:, None]).astype(jnp.float32)
    summed = jnp.dot(membership, per_token, precision=lax.Precision.HIGHEST, preferred_element_type=jnp.float32) / R
    positions = (jnp.arange(QSHARDS, dtype=jnp.int32)[:, None] * QPD + query_ids).reshape(-1).astype(jnp.int32)
    scores = jnp.take(summed, positions, axis=1)
    return input_grad, scores
```

```python
import jax
import jax.numpy as jnp
from jax import lax
from jax.sharding import PartitionSpec as P


EXAMPLES = 16
CHUNKS = 4


def shifted(value, axis, step):
    size = lax.axis_size(axis)
    return lax.ppermute(value, axis, [(i, (i + step) % size) for i in range(size)])


def contract_last(left_rows, right_rows, out_type=jnp.float32):
    return lax.dot_general(
        left_rows, right_rows, (((1,), (1,)), ((), ())), preferred_element_type=jnp.float32
    ).astype(out_type)


def silu_slope(preact, grad_part):
    sigmoid_value = jax.nn.sigmoid(preact)
    return (
        grad_part.astype(jnp.float32) * sigmoid_value * (1.0 + preact * (1.0 - sigmoid_value))
    ).astype(jnp.bfloat16)


def total_over(value, axis):
    parts = [shifted(value, axis, step) for step in range(1, lax.axis_size(axis))]
    for part in parts:
        value = value + part
    return value


def right_parts(features, right_factors, gate):
    queries, tensors = lax.axis_size("query"), lax.axis_size("tensor")
    query_index, tensor_index = lax.axis_index("query"), lax.axis_index("tensor")
    fold = tensors // queries
    width = right_factors.shape[2]
    flat = right_factors.reshape(-1, width)
    piece = lax.dynamic_slice_in_dim(features, tensor_index % fold * width, width, 1)
    rows = piece.shape[0] // tensors
    holder = (tensor_index // fold == query_index).astype(jnp.float32)
    moved = [shifted(flat, "query", step) for step in range(1, queries)]
    factors = [flat] + moved
    factors, _ = lax.optimization_barrier((factors, gate))
    part = contract_last(piece, jnp.concatenate(factors, axis=0)) * holder
    block = lax.dynamic_slice_in_dim(part, tensor_index * rows, rows, 0)
    for hop in range(1, tensors):
        send = lax.dynamic_slice_in_dim(part, (tensor_index + hop) % tensors * rows, rows, 0)
        moved = shifted(send, "tensor", hop)
        block = block + moved
    return jnp.split(block, queries, axis=1)


def right_whole(total):
    tensors, tensor_index = lax.axis_size("tensor"), lax.axis_index("tensor")
    rows = total.shape[0]
    others = [shifted(total, "tensor", hop) for hop in range(1, tensors)]
    turned = (others[::-1] + [total]) * 2
    return lax.dynamic_slice_in_dim(
        jnp.concatenate(turned, axis=0), (tensors - 1 - tensor_index) * rows, tensors * rows, 0
    )


def scatter_blocks(input_part, rows):
    tensors, cores = lax.axis_size("tensor"), lax.axis_size("dp")
    tensor_index, core = lax.axis_index("tensor"), lax.axis_index("dp")
    per_core = tensors // cores
    width = input_part.shape[1] // per_core
    parts = []
    for step in range(tensors):
        pick = (tensor_index + step) % tensors
        block = lax.dynamic_slice(
            input_part,
            ((core - pick % cores) % cores * rows, pick // cores * width),
            (rows, width),
        )
        perm = []
        for t in range(tensors):
            for d in range(cores):
                k = (t + step) % tensors
                perm.append((t * cores + d, (d * per_core + k // cores) * cores + k % cores))
        parts.append(lax.ppermute(block, ("tensor", "dp"), perm))
    return parts


def add_blocks(parts):
    total = parts[0].astype(jnp.float32)
    for part in parts[1:]:
        total = total + part.astype(jnp.float32)
    return total.astype(jnp.bfloat16)


def local(features, up_weight, out_grad, left_factors, right_factors, token_ids, query_ids):
    query_count, rank_count = left_factors.shape[0], left_factors.shape[1]
    cores, queries = lax.axis_size("dp"), lax.axis_size("query")
    core = lax.axis_index("dp")
    depth = up_weight.shape[0]
    tokens = features.shape[0]
    rows = tokens // CHUNKS
    flat_left = left_factors.reshape(query_count * rank_count, left_factors.shape[2])

    sets = [lax.dynamic_slice_in_dim(features, core * depth, depth, 1)]
    for step in range(1, cores):
        piece = lax.dynamic_slice_in_dim(features, (core + step) % cores * depth, depth, 1)
        sets.append(shifted(piece, "dp", step))

    sums, received, backs = [], [], []
    partials, sends = [], []
    for c in range(CHUNKS):
        span = slice(c * rows, (c + 1) * rows)
        stacked = jnp.concatenate([part[span] for part in sets], axis=0)
        partial = jnp.dot(stacked, up_weight, preferred_element_type=jnp.float32).astype(
            jnp.bfloat16
        )
        partials.append(partial)
        pieces = [partial[step * rows : (step + 1) * rows] for step in range(1, cores)]
        backs.append([shifted(piece, "dp", cores - i - 1) for i, piece in enumerate(pieces)])
    for c in range(CHUNKS):
        if c + 1 < CHUNKS:
            backs[c], _ = lax.optimization_barrier((backs[c], partials[c + 1]))
        own = partials[c][:rows].astype(jnp.float32)
        for back in backs[c]:
            own = own + back.astype(jnp.float32)
        send = own.astype(jnp.bfloat16)
        sends.append(send)
        if c == CHUNKS - 1:
            blocks = right_parts(features, right_factors, received_gate)
            send, blocks = lax.optimization_barrier((send, blocks))
            right_total = blocks[0]
            for step in range(1, queries):
                moved = shifted(blocks[step], "query", queries - step)
                right_total = right_total + moved
        sums.append(own)
        received.append([shifted(send, "query", step) for step in range(1, queries)])
        received_gate = send

    outputs, projections = [], []
    gate, waiting = (partials[-1], sends), None
    for c in range(CHUNKS):
        span = slice(c * rows, (c + 1) * rows)
        parts, _ = lax.optimization_barrier((received[c], gate))
        preact = sums[c]
        for part in parts:
            preact = preact + part.astype(jnp.float32)
        grad_rows = silu_slope(preact, out_grad[span])
        others = [shifted(grad_rows, "dp", step) for step in range(1, cores)]
        stacked = jnp.concatenate([grad_rows] + others, axis=0)
        input_part = contract_last(stacked, up_weight, jnp.bfloat16)
        if waiting is not None:
            waiting, _ = lax.optimization_barrier((waiting, input_part))
            outputs.append(add_blocks(waiting))
        waiting = scatter_blocks(input_part, rows)
        gate = input_part
        projections.append(contract_last(grad_rows, flat_left))
    right_sum = right_whole(right_total)
    outputs.append(add_blocks(waiting))
    input_grad = jnp.concatenate(outputs, axis=0)

    left_part = jnp.concatenate(projections, axis=0)
    per_token = (left_part * right_sum).reshape(-1, query_count, rank_count).sum(axis=-1)
    membership = (token_ids[None, :] == jnp.arange(EXAMPLES, dtype=jnp.int32)[:, None]).astype(
        jnp.float32
    )
    summed = jnp.dot(
        membership, per_token, precision=lax.Precision.HIGHEST, preferred_element_type=jnp.float32
    )
    column_order = (
        query_ids[0][:, None] == jnp.arange(query_count, dtype=jnp.int32)[None, :]
    ).astype(jnp.float32)
    ordered = lax.dot_general(
        summed,
        column_order,
        (((1,), (1,)), ((), ())),
        precision=lax.Precision.HIGHEST,
        preferred_element_type=jnp.float32,
    )
    scores = total_over(ordered / rank_count, "dp")
    scores, _ = lax.optimization_barrier((scores, input_part))
    scores = total_over(scores, "tensor")
    return (input_grad, scores)


def solution(mesh):
    return jax.shard_map(
        local,
        mesh=mesh,
        in_specs=(
            P(("groups", "dp"), "query"),
            P(("query", "dp"), "tensor"),
            P(("groups", "dp"), "tensor"),
            P("query", None, "tensor"),
            P("query", None, "tensor"),
            P(("groups", "dp")),
            P("query", None),
        ),
        out_specs=(P(("groups", "dp"), ("query", "tensor")), P("groups", "query")),
        check_vma=False,
    )
```
